256 devices in a mesh: seq: 32 (over x, y, core), tensor: 8 (over z).
Axes of the slice: x: 4, y: 4, z: 8, core: 2. Of those that a mesh axis runs over, the one named last changes fastest.
Arguments:
- tokens: bfloat16 [16384, 4096], P('seq', 'tensor'), may hold values from -6 to 6
- norm_gain: float32 [4096], replicated, may hold values from 0.1 to 1.9
- w_query: bfloat16 [4096, 4096], P('seq', 'tensor'), may hold values from -0.09375 to 0.09375
- w_key: bfloat16 [4096, 4096], P('seq', 'tensor'), may hold values from -0.09375 to 0.09375
- w_value: bfloat16 [4096, 4096], P('seq', 'tensor'), may hold values from -0.09375 to 0.09375
- out_gain: float32 [4096], P('tensor'), may hold values from 0.1 to 1.9
- carried: float32 [32, 128, 128], P('tensor'), may hold values from -384 to 384
Outputs:
- attended: bfloat16 [16384, 4096], P('seq', 'tensor')
- final_state: float32 [32, 128, 128], P('tensor')
The draws below stay inside these ranges and needn't reach their ends.
All inputs are finite; a program needn't handle non-finite values.
Results may differ from the reference program's by a relative error of at most 0.009.
Values may be sent and summed in bfloat16 or wider, within the bound.
No kernel may reach another device: no remote copies, remote signals or barrier semaphores. Data moves between devices by JAX's collectives and lax.ppermute only.
A program may use at most 64 MiB of HBM per device.

```python
import jax
import jax.numpy as jnp
from jax import lax

D = 4096
H = 32
HD = 128
BLOCK = 512
TOKENS = 16384


def block_scale(own_key, shape, shards, least, high):
    level = 1.0
    for axis_at, blocks in shards:
        steps = jax.random.uniform(jax.random.fold_in(jax.random.fold_in(own_key, 6), axis_at), (blocks,), jnp.float32, least / len(shards), high / len(shards))
        level = level * jnp.repeat(jnp.exp(steps), shape[axis_at] // blocks).reshape((-1,) + (1,) * (len(shape) - 1 - axis_at))
    return level


def bell_draw(rng, shape, deviation, reach, pieces=(), kind=jnp.bfloat16):
    result = deviation * jax.random.normal(rng, shape, jnp.float32)
    if pieces:
        result = result * block_scale(rng, shape, pieces, -0.22, 0.18)
    return jnp.clip(result, -reach, reach).astype(kind)


def setup_inputs(seed: int = 0) -> dict:
    key_list = jax.random.split(jax.random.key(seed), 8)
    return {
        "tokens": bell_draw(key_list[0], (TOKENS, D), 1.0, 6.0, ((0, 32), (1, 8))),
        "norm_gain": jnp.clip(1.0 + 0.18 * jax.random.normal(key_list[1], (D,), jnp.float32), 0.1, 1.9),
        "w_query": bell_draw(key_list[2], (D, H * HD), D ** -0.5, 0.09375, ((0, 32), (1, 8))),
        "w_key": bell_draw(key_list[3], (D, H * HD), D ** -0.5, 0.09375, ((0, 32), (1, 8))),
        "w_value": bell_draw(key_list[4], (D, H * HD), D ** -0.5, 0.09375, ((0, 32), (1, 8))),
        "out_gain": jnp.clip(1.0 + 0.18 * jax.random.normal(key_list[5], (H * HD,), jnp.float32), 0.1, 1.9),
        "carried": bell_draw(key_list[6], (H, HD, HD), 64.0, 384.0, ((0, 8),), jnp.float32),
    }


def reference(tokens, norm_gain, w_query, w_key, w_value, out_gain, carried):
    xf = tokens.astype(jnp.float32)
    normed = (xf * lax.rsqrt(lax.optimization_barrier(jnp.mean(xf * xf, axis=1, keepdims=True)) + 1e-05) * norm_gain).astype(jnp.bfloat16)
    query = jnp.dot(normed, w_query, preferred_element_type=jnp.float32).astype(jnp.bfloat16)
    key = jnp.dot(normed, w_key, preferred_element_type=jnp.float32).astype(jnp.bfloat16)
    value = jnp.dot(normed, w_value, preferred_element_type=jnp.float32).astype(jnp.bfloat16)
    count = TOKENS // BLOCK
    query = query.reshape(count, BLOCK, H, HD).transpose(2, 0, 1, 3)
    key = key.reshape(count, BLOCK, H, HD).transpose(2, 0, 1, 3)
    value = value.reshape(count, BLOCK, H, HD).transpose(2, 0, 1, 3)
    gains = out_gain.reshape(H, HD)
    causal = jnp.tril(jnp.ones((BLOCK, BLOCK), jnp.float32))

    def one_head(packed):
        qh, kh, vh, start, gain = packed

        def step(state, blocks):
            qb, kb, vb = blocks
            inter = jnp.dot(qb.astype(jnp.float32), state, precision=lax.Precision.HIGHEST)
            scores = (jnp.dot(qb, kb.T, preferred_element_type=jnp.float32) * causal).astype(jnp.bfloat16)
            raw = inter + jnp.dot(scores, vb, preferred_element_type=jnp.float32)
            out = raw * lax.rsqrt(lax.optimization_barrier(jnp.mean(raw * raw, axis=1, keepdims=True)) + 1e-06) * gain
            state = state + jnp.dot(kb.T, vb, preferred_element_type=jnp.float32)
            return (state, out.astype(jnp.bfloat16))
        state, outs = lax.scan(step, start, (qh, kh, vh))
        return (outs, state)
    outs, states = lax.map(one_head, (query, key, value, carried, gains))
    attended = outs.transpose(1, 2, 0, 3).reshape(TOKENS, H * HD)
    return (attended, states)
```

```python
import functools

import jax
import jax.numpy as jnp
from jax import lax
from jax.experimental import pallas as pl
from jax.experimental.pallas import tpu as pltpu
from jax.sharding import PartitionSpec as P

NX, NY, NC, NZ = 4, 4, 2, 8
BOTH = ("seq", "tensor")
BF, F32 = jnp.bfloat16, jnp.float32
OFFSETS = (0, 1, -1, 2)


def place(x, y, c, z):
    return (((x % NX) * NY + y % NY) * NC + c % NC) * NZ + z % NZ


def move(a, f):
    pairs = [
        (place(x, y, c, z), place(*f(x, y, c, z)))
        for x in range(NX)
        for y in range(NY)
        for c in range(NC)
        for z in range(NZ)
    ]
    return lax.ppermute(a, BOTH, pairs)


def swap(a):
    return move(a, lambda x, y, c, z: (x, y, c + 1, z))


def along_z(a):
    return move(a, lambda x, y, c, z: (x, y, c, z + (1 if c == 0 else -1)))


def first(a, k):
    return move(a, lambda x, y, c, z: (x + k, y, c, z) if c == 0 else (x, y + k, c, z))


def second(a, k):
    return move(a, lambda x, y, c, z: (x, y + k, c, z) if c == 0 else (x + k, y, c, z))


def by_x(a, k):
    return move(a, lambda x, y, c, z: (x + k, y, c, z))


def by_y(a, k):
    return move(a, lambda x, y, c, z: (x, y + k, c, z))


def gather_plane(a):
    stack = jnp.stack([a, first(a, 1), first(a, -1), first(a, 2)])
    right = second(stack, 1)
    left = second(stack, -1)
    far_a = second(right[:2], 1)
    far_b = second(left[2:], -1)
    return stack, right, left, far_a, far_b


def slots(parts):
    out = []
    for part, j, lo in ((0, 0, 0), (1, 1, 0), (2, 2, 0), (3, 3, 0), (4, 3, 2)):
        for n in range(parts[part].shape[0]):
            out.append((part, n, lo + n, j))
    return out


def row_block(c, x, y, i, j):
    d, e = OFFSETS[i], OFFSETS[j]
    qx = jnp.where(c == 0, x - d, x - e)
    qy = jnp.where(c == 0, y - e, y - d)
    return lax.rem(qx + NX, NX) * NY + lax.rem(qy + NY, NY)


def load_tokens(pos, pieces, x_s, sem):
    z, c = pos[2], pos[3]
    sign = 1 - 2 * c
    shifts = [0] + [-k for k in range(1, 5)] + [k for k in range(1, 4)]
    copies = []
    for piece, k in zip(pieces, shifts):
        at = lax.rem(z + sign * k + 2 * NZ, NZ)
        copies.append(
            pltpu.make_async_copy(piece, x_s.at[:, pl.ds(pl.multiple_of(at * 512, 512), 512)], sem)
        )
    return copies


def load_weights(pos, mine, other, w_s, sems):
    x, y, c = pos[0], pos[1], pos[3]
    groups = []
    for which, parts in enumerate((mine, other)):
        owner = c if which == 0 else 1 - c
        copies = []
        for part, n, i, j in slots(parts):
            q = row_block(owner, x, y, i, j)
            copies.append(
                pltpu.make_async_copy(
                    parts[part].at[n],
                    w_s.at[owner, pl.ds(pl.multiple_of(q * 256, 256), 256), :],
                    sems.at[which],
                )
            )
        groups.append(copies)
    return groups


def kv_kernel(pos, *refs):
    pieces, mine, other = refs[:8], refs[8:13], refs[13:18]
    kv_ref, r_ref, s_ref, x_s, w_s, sem_x, sem_w = refs[18:]
    loads = load_tokens(pos, pieces, x_s, sem_x)
    for cp in loads:
        cp.start()
    groups = load_weights(pos, mine, other, w_s, sem_w)
    for group in groups:
        for cp in group:
            cp.start()
    for cp in loads:
        cp.wait()
    total = jnp.zeros((512, 128), F32)
    for b in range(32):
        xb = x_s[:, b * 128 : (b + 1) * 128].astype(F32)
        total = total + xb * xb
    r = lax.rsqrt(jnp.sum(total, axis=1, keepdims=True) * (1.0 / 4096) + 1e-05)
    r_ref[...] = jnp.broadcast_to(r, (512, 128))
    for group in groups:
        for cp in group:
            cp.wait()

    @pl.loop(0, 4)
    def _(i):
        lanes = pl.ds(pl.multiple_of((i % 2) * 256, 256), 256)
        got = jnp.dot(x_s[...], w_s[i // 2, :, lanes], preferred_element_type=F32)
        kv_ref[i // 2, :, lanes] = (got * r_ref[:, :1]).astype(BF)

    @pl.loop(0, 4)
    def _(h):
        lanes = pl.ds(pl.multiple_of(h * 128, 128), 128)
        s_ref[h] = lax.dot_general(
            kv_ref[0, :, lanes],
            kv_ref[1, :, lanes],
            (((0,), (0,)), ((), ())),
            preferred_element_type=F32,
        )


def split_dot(q, m):
    hi = m.astype(BF)
    lo = (m - hi.astype(F32)).astype(BF)
    return jnp.dot(q, hi, preferred_element_type=F32) + jnp.dot(q, lo, preferred_element_type=F32)


def q_kernel(pos, *refs):
    pieces, mine, other = refs[:8], refs[8:13], refs[13:18]
    kv_ref, r_ref, carried_ref, q_ref, raw_ref, x_s, w_s, sem_x, sem_w = refs[18:]
    loads = load_tokens(pos, pieces, x_s, sem_x)
    for cp in loads:
        cp.start()
    groups = load_weights(pos, mine, other, w_s, sem_w)
    for group in groups:
        for cp in group:
            cp.start()
    for cp in loads:
        cp.wait()
    for group in groups:
        for cp in group:
            cp.wait()
    row = lax.broadcasted_iota(jnp.int32, (512, 512), 0)
    col = lax.broadcasted_iota(jnp.int32, (512, 512), 1)

    @pl.loop(0, 2)
    def _(h):
        got = jnp.dot(x_s[...], w_s[h], preferred_element_type=F32)
        q_ref[:, pl.ds(pl.multiple_of(h * 256, 256), 256)] = (got * r_ref[:, :1]).astype(BF)

    @pl.loop(0, 4)
    def _(h):
        lanes = pl.ds(pl.multiple_of(h * 128, 128), 128)
        q = q_ref[:, lanes]
        scores = lax.dot_general(
            q, kv_ref[0, :, lanes], (((1,), (1,)), ((), ())), preferred_element_type=F32
        )
        weights = jnp.where(col <= row, scores, 0.0).astype(BF)
        intra = jnp.dot(weights, kv_ref[1, :, lanes], preferred_element_type=F32)
        raw_ref[:, lanes] = intra + split_dot(q, carried_ref[h])


def out_kernel(q_ref, raw_ref, before_ref, gain_ref, out_ref):
    for h in range(4):
        lanes = slice(h * 128, (h + 1) * 128)
        raw = raw_ref[:, lanes] + split_dot(q_ref[:, lanes], before_ref[h])
        scale = lax.rsqrt(jnp.mean(raw * raw, axis=1, keepdims=True) + 1e-06)
        out_ref[:, lanes] = (raw * scale * gain_ref[:, lanes]).astype(BF)


SMEM = pl.BlockSpec(memory_space=pltpu.SMEM)
ANY = pl.BlockSpec(memory_space=pl.ANY)
VMEM = pl.BlockSpec(memory_space=pltpu.VMEM)
LIMIT = pltpu.CompilerParams(vmem_limit_bytes=40 << 20)


def shards(tokens, norm_gain, w_query, w_key, w_value, out_gain, carried):
    s = lax.axis_index("seq").astype(jnp.int32)
    z = lax.axis_index("tensor").astype(jnp.int32)
    c = s % 2
    y = (s // 2) % NY
    x = s // (2 * NY)
    pos = jnp.stack([x, y, z, c])
    even = c == 0

    sib = swap(tokens)
    own_chain, sib_chain = [tokens], [sib]
    for k in range(3):
        own_chain.append(along_z(own_chain[-1]))
        sib_chain.append(along_z(sib_chain[-1]))
    own_chain.append(along_z(own_chain[-1]))
    pieces = own_chain + [swap(b) for b in sib_chain[1:]]

    g = lax.dynamic_slice(norm_gain, (s * 128,), (128,))[:, None]
    scaled = lambda w: (w.astype(F32) * g).astype(BF)
    wq, wk, wv = scaled(w_query), scaled(w_key), scaled(w_value)
    pick = lambda a, b: jnp.where(even, a, b)
    mine = jnp.concatenate([pick(wk, wv), pick(wq[:, :256], wq[:, 256:])], 1)
    give = jnp.concatenate([pick(wv, wk), pick(wq[:, 256:], wq[:, :256])], 1)
    got = swap(give)
    chip = jnp.concatenate([pick(mine, got), pick(got, mine)], 0)
    kv = gather_plane(chip[:, :512])
    qq = gather_plane(chip[:, 512:])
    kv_other = [swap(a) for a in kv]
    qq_other = [swap(a) for a in qq]

    flops = 2 * 512 * 4096 * 1024
    kv_rows, r, state = pl.pallas_call(
        kv_kernel,
        name="kv",
        out_shape=(
            jax.ShapeDtypeStruct((2, 512, 512), BF),
            jax.ShapeDtypeStruct((512, 128), F32),
            jax.ShapeDtypeStruct((4, 128, 128), F32),
        ),
        in_specs=[SMEM] + [ANY] * 18,
        out_specs=(VMEM,) * 3,
        scratch_shapes=[
            pltpu.VMEM((512, 4096), BF),
            pltpu.VMEM((2, 4096, 512), BF),
            pltpu.SemaphoreType.DMA,
            pltpu.SemaphoreType.DMA((2,)),
        ],
        compiler_params=LIMIT,
        cost_estimate=pl.CostEstimate(flops=flops, bytes_accessed=13 << 20, transcendentals=0),
    )(pos, *pieces, *kv, *kv_other)

    query, raw = pl.pallas_call(
        q_kernel,
        name="q",
        out_shape=(
            jax.ShapeDtypeStruct((512, 512), BF),
            jax.ShapeDtypeStruct((512, 512), F32),
        ),
        in_specs=[SMEM] + [ANY] * 18 + [VMEM] * 3,
        out_specs=(VMEM,) * 2,
        scratch_shapes=[
            pltpu.VMEM((512, 4096), BF),
            pltpu.VMEM((2, 4096, 256), BF),
            pltpu.SemaphoreType.DMA,
            pltpu.SemaphoreType.DMA((2,)),
        ],
        compiler_params=LIMIT,
        cost_estimate=pl.CostEstimate(flops=flops, bytes_accessed=10 << 20, transcendentals=0),
    )(pos, *pieces, *qq, *qq_other, kv_rows, r, carried)

    low, high = state[:2], state[2:]
    part = pick(low, high)
    from_sib = swap(pick(high, low).astype(BF)).astype(F32)
    chip_state = part + from_sib

    def across(a, go, at):
        sent = a.astype(BF)
        near = [go(sent, 1), go(sent, -1), go(sent, 2)]
        b, f, o = [n.astype(F32) for n in near]
        total = (lax.reduce_precision(a, 8, 7) + o) + (b + f)
        before = jnp.where(at >= 1, b, 0.0)
        before = before + jnp.where(at >= 2, o, 0.0) + jnp.where(at == 3, f, 0.0)
        return before, total

    before_y, row_total = across(chip_state, by_y, y)
    before_x, total = across(row_total, by_x, x)
    before = before_x + before_y
    mine_before = before + jnp.where(even, 0.0, from_sib)
    give_before = before + jnp.where(even, part, 0.0)
    both = swap(jnp.stack([give_before, total]))
    order = lambda a, b: jnp.concatenate([pick(a, b), pick(b, a)], 0)
    before_all = order(mine_before, both[0])
    total_all = order(total, both[1])

    attended = pl.pallas_call(
        out_kernel,
        name="out",
        out_shape=jax.ShapeDtypeStruct((512, 512), BF),
        in_specs=[VMEM] * 4,
        out_specs=VMEM,
        compiler_params=LIMIT,
        cost_estimate=pl.CostEstimate(flops=1 << 28, bytes_accessed=2 << 20, transcendentals=0),
    )(query, raw, before_all, out_gain.reshape(1, 512))
    return attended, carried + total_all


def solution(mesh):
    return jax.shard_map(
        shards,
        mesh=mesh,
        in_specs=(
            P("seq", "tensor"),
            P(),
            P("seq", "tensor"),
            P("seq", "tensor"),
            P("seq", "tensor"),
            P("tensor"),
            P("tensor", None, None),
        ),
        out_specs=(P("seq", "tensor"), P("tensor", None, None)),
        check_vma=False,
    )
```

```python
import jax
import jax.numpy as jnp
from jax import lax
from jax.experimental import pallas as pl
from jax.experimental.pallas import tpu as pltpu
from jax.sharding import PartitionSpec as P

NX, NY, NC, NZ = 4, 4, 2, 8
BOTH = ("seq", "tensor")
BF, F32 = jnp.bfloat16, jnp.float32


def place(x, y, c, z):
    return (((x % NX) * NY + y % NY) * NC + c % NC) * NZ + z % NZ


def move(a, f):
    pairs = [
        (place(x, y, c, z), place(*f(x, y, c, z)))
        for x in range(NX)
        for y in range(NY)
        for c in range(NC)
        for z in range(NZ)
    ]
    return lax.ppermute(a, BOTH, pairs)


def swap(a):
    return move(a, lambda x, y, c, z: (x, y, c + 1, z))


def along_z(a):
    return move(a, lambda x, y, c, z: (x, y, c, z + (1 if c == 0 else -1)))


def first(a, k):
    return move(a, lambda x, y, c, z: (x + k, y, c, z) if c == 0 else (x, y + k, c, z))


def second(a, k):
    return move(a, lambda x, y, c, z: (x, y + k, c, z) if c == 0 else (x + k, y, c, z))


def by_x(a, k):
    return move(a, lambda x, y, c, z: (x + k, y, c, z))


def by_y(a, k):
    return move(a, lambda x, y, c, z: (x, y + k, c, z))


def scalars(pos):
    return pos[0], pos[1], pos[2], pos[3]


def slot_of(step):
    step = lax.rem(step + 4, 4)
    return jnp.where(step >= 2, 5 - step, step)


def column(c, x, y, q):
    dx, dy = slot_of(x - q // NY), slot_of(y - lax.rem(q, NY))
    return jnp.where(c == 0, dy * 4 + dx, dx * 4 + dy)


def weights_dot(x_ref, parts, lanes):
    acc = None
    at = 0
    for part, n in parts:
        d = jnp.dot(x_ref[:, at : at + n], part[:n, lanes], preferred_element_type=F32)
        acc = d if acc is None else acc + d
        at += n
    return acc


def kv_kernel(pos, own, z1, z2, z3, a4, st, right, left, far_a, far_b, got_a, got_b, got_c, *outs):
    kv_ref, r_ref, part_ref, give_ref, xa_ref, xb_ref = outs
    mine = ((st, 1024), (right, 1024), (left, 1024), (far_a, 512), (far_b, 512))
    other = ((got_a, 1024), (got_b, 2048), (got_c, 1024))
    pieces = (
        (own, 0), (z1, 0), (z2, 0), (z3, 0), (a4, 0), (got_a, 1024), (got_b, 2048), (got_c, 1024)
    )
    x, y, z, c = scalars(pos)
    sign = 1 - 2 * c
    shifts = [0] + [-k for k in range(1, 5)] + [k for k in range(1, 4)]
    total = jnp.zeros((512, 128), F32)
    for (piece, lo), k in zip(pieces, shifts):
        at = lax.rem(z + sign * k + 2 * NZ, NZ)
        for h in range(2):
            q = 2 * at + h
            block = piece[lo : lo + 512, h * 256 : (h + 1) * 256]
            xa_ref[:, pl.ds(pl.multiple_of(column(c, x, y, q) * 256, 256), 256)] = block
            xb_ref[:, pl.ds(pl.multiple_of(column(1 - c, x, y, q) * 256, 256), 256)] = block
            wide = block.astype(F32)
            wide = wide * wide
            total = total + wide[:, :128] + wide[:, 128:]
    r = lax.rsqrt(jnp.sum(total, axis=1, keepdims=True) * (1.0 / 4096) + 1e-05)
    r_ref[...] = jnp.broadcast_to(r, (512, 128))

    @pl.loop(0, 2)
    def _(i):
        lanes = pl.ds(pl.multiple_of(i * 256, 256), 256)
        kv_ref[c, :, lanes] = (weights_dot(xa_ref, mine, lanes) * r_ref[:, :1]).astype(BF)
        kv_ref[1 - c, :, lanes] = (weights_dot(xb_ref, other, lanes) * r_ref[:, :1]).astype(BF)

    @pl.loop(0, 4)
    def _(h):
        head = lax.rem(h + 2 * c, 4)
        lanes = pl.ds(pl.multiple_of(head * 128, 128), 128)
        state = lax.dot_general(
            kv_ref[0, :, lanes],
            kv_ref[1, :, lanes],
            (((0,), (0,)), ((), ())),
            preferred_element_type=F32,
        )

        @pl.when(h < 2)
        def _():
            part_ref[h] = state

        @pl.when(h >= 2)
        def _():
            give_ref[h - 2] = state.astype(BF)


def chip_kernel(pos, part_ref, sib_ref, sent_ref):
    sent_ref[...] = (part_ref[...] + sib_ref[...].astype(F32)).astype(BF)


def along(at, sent, behind, ahead, opposite):
    b, f, o = behind[...].astype(F32), ahead[...].astype(F32), opposite[...].astype(F32)
    total = (sent[...].astype(F32) + o) + (b + f)
    before = jnp.where(at >= 1, b, 0.0) + jnp.where(at >= 2, o, 0.0) + jnp.where(at == 3, f, 0.0)
    return before, total


def row_kernel(pos, sent, behind, ahead, opposite, before_ref, next_ref):
    before, total = along(pos[1], sent, behind, ahead, opposite)
    before_ref[...] = before
    next_ref[...] = total.astype(BF)


def plane_kernel(pos, sent, behind, ahead, opposite, row_ref, part_ref, sib_ref, mine_ref, both_ref):
    before, total = along(pos[0], sent, behind, ahead, opposite)
    before = before + row_ref[...]
    c = pos[3]
    mine_ref[0] = before + jnp.where(c == 1, sib_ref[...].astype(F32), 0.0)
    mine_ref[1] = total
    both_ref[0] = before + jnp.where(c == 0, part_ref[...], 0.0)
    both_ref[1] = total


def split_dot(q, m):
    hi = m.astype(BF)
    lo = (m - hi.astype(F32)).astype(BF)
    return jnp.dot(q, hi, preferred_element_type=F32) + jnp.dot(q, lo, preferred_element_type=F32)


def q_kernel(pos, xa_ref, xb_ref, *refs):
    sizes = (1024, 1024, 1024, 512, 512, 3072, 1024)
    parts = tuple(zip(refs[:7], sizes))
    mine, other = parts[:5], parts[5:]
    kv_ref, r_ref, carried_ref, q_ref, raw_ref = refs[7:]
    c = pos[3]
    for x_ref, parts, to in ((xa_ref, mine, c), (xb_ref, other, 1 - c)):
        got = weights_dot(x_ref, parts, slice(0, 256)) * r_ref[:, :1]
        q_ref[:, pl.ds(pl.multiple_of(to * 256, 256), 256)] = got.astype(BF)
    row = lax.broadcasted_iota(jnp.int32, (512, 512), 0)
    col = lax.broadcasted_iota(jnp.int32, (512, 512), 1)

    @pl.loop(0, 4)
    def _(h):
        lanes = pl.ds(pl.multiple_of(h * 128, 128), 128)
        q = q_ref[:, lanes]
        scores = lax.dot_general(
            q, kv_ref[0, :, lanes], (((1,), (1,)), ((), ())), preferred_element_type=F32
        )
        weights = jnp.where(col <= row, scores, 0.0).astype(BF)
        intra = jnp.dot(weights, kv_ref[1, :, lanes], preferred_element_type=F32)
        raw_ref[:, lanes] = intra + split_dot(q, carried_ref[h])


def out_kernel(pos, q_ref, raw_ref, mine_ref, both_ref, carried_ref, gain_ref, out_ref, final_ref):
    c = pos[3]
    for own in range(2):
        for n in range(2):
            h = 2 * (c if own else 1 - c) + n
            lanes = pl.ds(pl.multiple_of(h * 128, 128), 128)
            before = mine_ref[0, n] if own else both_ref[0, n]
            total = mine_ref[1, n] if own else both_ref[1, n]
            raw = raw_ref[:, lanes] + split_dot(q_ref[:, lanes], before)
            scale = lax.rsqrt(jnp.mean(raw * raw, axis=1, keepdims=True) + 1e-06)
            out_ref[:, lanes] = (raw * scale * gain_ref[:, lanes]).astype(BF)
            final_ref[h] = carried_ref[h] + total


SMEM = pl.BlockSpec(memory_space=pltpu.SMEM)
VMEM = pl.BlockSpec(memory_space=pltpu.VMEM)


def kernel(body, name, outs, n_in, flops, space=VMEM, scratch=(), spaces=None, size=8):
    return pl.pallas_call(
        body,
        name=name,
        out_shape=tuple(jax.ShapeDtypeStruct(*o) for o in outs),
        in_specs=[SMEM] + (space if isinstance(space, list) else [space] * n_in),
        out_specs=tuple(spaces or [VMEM] * len(outs)),
        scratch_shapes=scratch,
        compiler_params=pltpu.CompilerParams(vmem_limit_bytes=size << 20),
        cost_estimate=pl.CostEstimate(flops=flops, bytes_accessed=1 << 20, transcendentals=0),
    )


def after(a, *deps):
    return lax.optimization_barrier((a,) + deps)[0]


def shards(tokens, norm_gain, w_query, w_key, w_value, out_gain, carried):
    s = lax.axis_index("seq").astype(jnp.int32)
    z = lax.axis_index("tensor").astype(jnp.int32)
    c = lax.rem(s, 2)
    y = lax.rem(s // 2, NY)
    x = s // (2 * NY)
    pos = jnp.stack([x, y, z, c])
    tokens, pos = lax.optimization_barrier((tokens, pos))
    even = c == 0
    pick = lambda a, b: jnp.where(even, a, b)

    sib = swap(tokens)
    g = lax.dynamic_slice(norm_gain, (s * 128,), (128,))[:, None]
    scaled = lambda w: (w.astype(F32) * g).astype(BF)
    wq, wk, wv = scaled(w_query), scaled(w_key), scaled(w_value)
    qa, qb = wq[:, :256], wq[:, 256:]
    mine = jnp.concatenate([pick(wk, wv), pick(qa, qb)], 1)
    give = jnp.concatenate([pick(wv, wk), pick(qb, qa)], 1)
    got = swap(after(give, sib))
    chip = jnp.concatenate([pick(mine, got), pick(got, mine)], 0)
    cat = jnp.concatenate
    z1 = along_z(after(cat([tokens, sib]), got))
    near = [first(chip, k) for k in (1, -1, 2)]
    z1, *near = lax.optimization_barrier((z1, *near))
    near = [chip] + near
    st = cat([w[:, :512] for w in near])
    qst = cat([w[:, 512:] for w in near])
    z2 = along_z(z1)
    right, left = second(st, 1), second(st, -1)
    got_a = swap(cat([st, z1[512:]]))
    z2, right, left, got_a = lax.optimization_barrier((z2, right, left, got_a))
    z3 = along_z(z2)
    far_a, far_b = second(right[:512], 1), second(left[512:], -1)
    got_b = swap(cat([right, left, z2[512:]]))
    z3, far_a, far_b, got_b = lax.optimization_barrier((z3, far_a, far_b, got_b))
    a4 = along_z(z3[:512])
    qright, qleft = second(qst, 1), second(qst, -1)
    got_c = swap(cat([far_a, far_b, z3[512:]]))
    a4, qright, qleft, got_c = lax.optimization_barrier((a4, qright, qleft, got_c))
    qfar_a, qfar_b = second(qright[:512], 1), second(qleft[512:], -1)
    q_parts = (qst, qright, qleft, qfar_a, qfar_b)

    flops = 2 * 512 * 4096 * 1024
    kv_rows, r, part, give, xa, xb = kernel(
        kv_kernel,
        "kv",
        [
            ((2, 512, 512), BF),
            ((512, 128), F32),
            ((2, 128, 128), F32),
            ((2, 128, 128), BF),
            ((512, 4096), BF),
            ((512, 4096), BF),
        ],
        13,
        flops,
    )(pos, tokens, z1, z2, z3, a4, st, right, left, far_a, far_b, got_a, got_b, got_c)
    q_other = (
        swap(cat([qst, qright, qleft])),
        swap(after(cat([qfar_a, after(qfar_b, part)]), part)),
    )
    query, raw = kernel(q_kernel, "q", [((512, 512), BF), ((512, 512), F32)], 12, flops)(
        pos, xa, xb, *q_parts, *q_other, kv_rows, r, carried
    )

    heads = (2, 128, 128)
    from_sib = swap(give)
    (sent,) = kernel(chip_kernel, "chip", [(heads, BF)], 2, 1 << 16)(
        pos, part, from_sib
    )
    near = [by_y(sent, k) for k in (1, -1, 2)]
    before, row = kernel(row_kernel, "row", [(heads, F32), (heads, BF)], 4, 1 << 16)(
        pos, sent, *near
    )
    near = [by_x(row, k) for k in (1, -1, 2)]
    before = after(before, raw)
    both = (2,) + heads
    mine, give = kernel(plane_kernel, "plane", [(both, F32), (both, F32)], 7, 1 << 16)(
        pos, row, *near, before, part, from_sib
    )
    return kernel(out_kernel, "out", [((512, 512), BF), ((4, 128, 128), F32)], 6, 1 << 28)(
        pos, query, raw, mine, swap(give), carried, out_gain.reshape(1, 512)
    )


def solution(mesh):
    return jax.shard_map(
        shards,
        mesh=mesh,
        in_specs=(
            P("seq", "tensor"),
            P(),
            P("seq", "tensor"),
            P("seq", "tensor"),
            P("seq", "tensor"),
            P("tensor"),
            P("tensor", None, None),
        ),
        out_specs=(P("seq", "tensor"), P("tensor", None, None)),
        check_vma=False,
    )
```

```python
import jax
import jax.numpy as jnp
from jax import lax
from jax.experimental import pallas as pl
from jax.experimental.pallas import tpu as pltpu
from jax.sharding import PartitionSpec as P

NX, NY, NC, NZ = 4, 4, 2, 8
BOTH = ("seq", "tensor")
BF, F32 = jnp.bfloat16, jnp.float32


def place(x, y, c, z):
    return (((x % NX) * NY + y % NY) * NC + c % NC) * NZ + z % NZ


def move(a, f):
    pairs = [
        (place(x, y, c, z), place(*f(x, y, c, z)))
        for x in range(NX)
        for y in range(NY)
        for c in range(NC)
        for z in range(NZ)
    ]
    return lax.ppermute(a, BOTH, pairs)


def swap(a):
    return move(a, lambda x, y, c, z: (x, y, c + 1, z))


def along_z(a):
    return move(a, lambda x, y, c, z: (x, y, c, z + (1 if c == 0 else -1)))


def first(a, k):
    return move(a, lambda x, y, c, z: (x + k, y, c, z) if c == 0 else (x, y + k, c, z))


def second(a, k):
    return move(a, lambda x, y, c, z: (x, y + k, c, z) if c == 0 else (x + k, y, c, z))


def by_x(a, k):
    return move(a, lambda x, y, c, z: (x + k, y, c, z))


def by_y(a, k):
    return move(a, lambda x, y, c, z: (x, y + k, c, z))


def scalars(pos):
    return pos[0], pos[1], pos[2], pos[3]


def slot_of(step):
    step = lax.rem(step + 4, 4)
    return jnp.where(step >= 2, 5 - step, step)


def column(c, x, y, q):
    dx, dy = slot_of(x - q // NY), slot_of(y - lax.rem(q, NY))
    return jnp.where(c == 0, dy * 4 + dx, dx * 4 + dy)


def weights_dot(x_ref, parts, lanes):
    acc = None
    at = 0
    for part, n in parts:
        d = jnp.dot(x_ref[:, at : at + n], part[:n, lanes], preferred_element_type=F32)
        acc = d if acc is None else acc + d
        at += n
    return acc


def x_pass(pos, pieces, xa_ref, xb_ref, total):
    x, y, z, c = scalars(pos)
    for piece, lo, k in pieces:
        at = lax.rem(z + (1 - 2 * c) * k + 2 * NZ, NZ)
        for h in range(2):
            q = 2 * at + h
            block = piece[lo : lo + 512, h * 256 : (h + 1) * 256]
            xa_ref[:, pl.ds(pl.multiple_of(column(c, x, y, q) * 256, 256), 256)] = block
            xb_ref[:, pl.ds(pl.multiple_of(column(1 - c, x, y, q) * 256, 256), 256)] = block
            wide = block.astype(F32)
            wide = wide * wide
            total = total + wide[:, :128] + wide[:, 128:]
    return total


def x_kernel(pos, own, z1, z2, z3, got_a, xa_ref, xb_ref, squares_ref):
    pieces = ((own, 0, 0), (z1, 0, -1), (z2, 0, -2), (z3, 0, -3), (got_a, 1024, 1))
    squares_ref[...] = x_pass(pos, pieces, xa_ref, xb_ref, jnp.zeros((512, 128), F32))


def kv_kernel(pos, xa_in, xb_in, squares, a4, st, right, left, far_a, far_b, got_a, got_b, *outs):
    kv_ref, r_ref, part_ref, give_ref, xa_ref, xb_ref = outs
    c = pos[3]
    mine = ((st, 1024), (right, 1024), (left, 1024), (far_a, 512), (far_b, 512))
    other = ((got_a, 1024), (got_b, 3072))
    pieces = ((a4, 0, -4), (got_b, 3072, 2), (got_b, 3584, 3))
    total = x_pass(pos, pieces, xa_ref, xb_ref, squares[...])
    r = lax.rsqrt(jnp.sum(total, axis=1, keepdims=True) * (1.0 / 4096) + 1e-05)
    r_ref[...] = jnp.broadcast_to(r, (512, 128))

    @pl.loop(0, 2)
    def _(i):
        lanes = pl.ds(pl.multiple_of(i * 256, 256), 256)
        kv_ref[c, :, lanes] = (weights_dot(xa_ref, mine, lanes) * r_ref[:, :1]).astype(BF)
        kv_ref[1 - c, :, lanes] = (weights_dot(xb_ref, other, lanes) * r_ref[:, :1]).astype(BF)

    @pl.loop(0, 4)
    def _(h):
        head = lax.rem(h + 2 * c, 4)
        lanes = pl.ds(pl.multiple_of(head * 128, 128), 128)
        state = lax.dot_general(
            kv_ref[0, :, lanes],
            kv_ref[1, :, lanes],
            (((0,), (0,)), ((), ())),
            preferred_element_type=F32,
        )

        @pl.when(h < 2)
        def _():
            part_ref[h] = state

        @pl.when(h >= 2)
        def _():
            give_ref[h - 2] = state.astype(BF)


def chip_kernel(pos, part_ref, sib_ref, sent_ref):
    sent_ref[...] = (part_ref[...] + sib_ref[...].astype(F32)).astype(BF)


def along(at, sent, behind, ahead, opposite):
    b, f, o = behind[...].astype(F32), ahead[...].astype(F32), opposite[...].astype(F32)
    total = (sent[...].astype(F32) + o) + (b + f)
    before = jnp.where(at >= 1, b, 0.0) + jnp.where(at >= 2, o, 0.0) + jnp.where(at == 3, f, 0.0)
    return before, total


def row_kernel(pos, sent, behind, ahead, opposite, before_ref, next_ref):
    before, total = along(pos[1], sent, behind, ahead, opposite)
    before_ref[...] = before
    next_ref[...] = total.astype(BF)


def plane_kernel(pos, sent, behind, ahead, opposite, row_ref, part_ref, sib_ref, mine_ref, both_ref):
    before, total = along(pos[0], sent, behind, ahead, opposite)
    before = before + row_ref[...]
    c = pos[3]
    mine_ref[0] = before + jnp.where(c == 1, sib_ref[...].astype(F32), 0.0)
    mine_ref[1] = total
    both_ref[0] = before + jnp.where(c == 0, part_ref[...], 0.0)
    both_ref[1] = total


def split_dot(q, m):
    hi = m.astype(BF)
    lo = (m - hi.astype(F32)).astype(BF)
    return jnp.dot(q, hi, preferred_element_type=F32) + jnp.dot(q, lo, preferred_element_type=F32)


def q_kernel(pos, xa_ref, xb_ref, *refs):
    sizes = (1024, 1024, 1024, 512, 512, 3072, 1024)
    parts = tuple(zip(refs[:7], sizes))
    mine, other = parts[:5], parts[5:]
    r_ref, q_ref = refs[7:]
    c = pos[3]
    for x_ref, parts, to in ((xa_ref, mine, c), (xb_ref, other, 1 - c)):
        got = weights_dot(x_ref, parts, slice(0, 256)) * r_ref[:, :1]
        q_ref[:, pl.ds(pl.multiple_of(to * 256, 256), 256)] = got.astype(BF)


def block_kernel(pos, q_ref, kv_ref, carried_ref, raw_ref):
    row = lax.broadcasted_iota(jnp.int32, (512, 512), 0)
    col = lax.broadcasted_iota(jnp.int32, (512, 512), 1)

    @pl.loop(0, 4)
    def _(h):
        lanes = pl.ds(pl.multiple_of(h * 128, 128), 128)
        q = q_ref[:, lanes]
        scores = lax.dot_general(
            q, kv_ref[0, :, lanes], (((1,), (1,)), ((), ())), preferred_element_type=F32
        )
        weights = jnp.where(col <= row, scores, 0.0).astype(BF)
        intra = jnp.dot(weights, kv_ref[1, :, lanes], preferred_element_type=F32)
        raw_ref[:, lanes] = intra + split_dot(q, carried_ref[h])


def out_kernel(pos, q_ref, raw_ref, mine_ref, both_ref, carried_ref, gain_ref, out_ref, final_ref):
    c = pos[3]
    for own in range(2):
        for n in range(2):
            h = 2 * (c if own else 1 - c) + n
            lanes = pl.ds(pl.multiple_of(h * 128, 128), 128)
            before = mine_ref[0, n] if own else both_ref[0, n]
            total = mine_ref[1, n] if own else both_ref[1, n]
            raw = raw_ref[:, lanes] + split_dot(q_ref[:, lanes], before)
            scale = lax.rsqrt(jnp.mean(raw * raw, axis=1, keepdims=True) + 1e-06)
            out_ref[:, lanes] = (raw * scale * gain_ref[:, lanes]).astype(BF)
            final_ref[h] = carried_ref[h] + total


SMEM = pl.BlockSpec(memory_space=pltpu.SMEM)
VMEM = pl.BlockSpec(memory_space=pltpu.VMEM)


def kernel(body, name, outs, n_in, flops, space=VMEM, scratch=(), aliases=None, size=8):
    return pl.pallas_call(
        body,
        name=name,
        out_shape=tuple(jax.ShapeDtypeStruct(*o) for o in outs),
        in_specs=[SMEM] + (space if isinstance(space, list) else [space] * n_in),
        out_specs=(VMEM,) * len(outs),
        input_output_aliases=aliases or {},
        scratch_shapes=scratch,
        compiler_params=pltpu.CompilerParams(vmem_limit_bytes=size << 20),
        cost_estimate=pl.CostEstimate(flops=flops, bytes_accessed=1 << 20, transcendentals=0),
    )


def after(a, *deps):
    return lax.optimization_barrier((a,) + deps)[0]


def shards(tokens, norm_gain, w_query, w_key, w_value, out_gain, carried):
    s = lax.axis_index("seq").astype(jnp.int32)
    z = lax.axis_index("tensor").astype(jnp.int32)
    c = lax.rem(s, 2)
    y = lax.rem(s // 2, NY)
    x = s // (2 * NY)
    pos = jnp.stack([x, y, z, c])
    tokens, pos = lax.optimization_barrier((tokens, pos))
    even = c == 0
    pick = lambda a, b: jnp.where(even, a, b)

    sib = swap(tokens)
    mine = jnp.concatenate([pick(w_key, w_value), pick(w_query[:, :256], w_query[:, 256:])], 1)
    give = jnp.concatenate([pick(w_value, w_key), pick(w_query[:, 256:], w_query[:, :256])], 1)
    got = swap(after(give, sib))
    g = lax.dynamic_slice(norm_gain, ((s // 2) * 256,), (256,))[:, None]
    chip = jnp.concatenate([pick(mine, got), pick(got, mine)], 0)
    chip = (chip.astype(F32) * g).astype(BF)
    cat = jnp.concatenate
    z1 = along_z(after(cat([tokens, sib]), got))
    near = [first(chip, k) for k in (1, -1, 2)]
    z1, *near = lax.optimization_barrier((z1, *near))
    near = [chip] + near
    st = cat([w[:, :512] for w in near])
    qst = cat([w[:, 512:] for w in near])
    z2 = along_z(z1)
    right, left = second(st, 1), second(st, -1)
    got_a = swap(cat([st, z1[512:]]))
    z2, right, left, got_a = lax.optimization_barrier((z2, right, left, got_a))
    z3 = along_z(z2)
    far_a, far_b = second(right[:512], 1), second(left[512:], -1)
    qright, qleft = second(qst, 1), second(qst, -1)
    z3, far_a, far_b, qright, qleft = lax.optimization_barrier((z3, far_a, far_b, qright, qleft))
    a4 = along_z(z3[:512])
    qfar_a, qfar_b = second(qright[:512], 1), second(qleft[512:], -1)
    got_b = swap(cat([right, left, far_a, far_b, z2[512:], z3[512:]]))
    got_q = swap(cat([qst, qright, qleft]))
    orders = [((512, 4096), BF), ((512, 4096), BF)]
    xa, xb, squares = kernel(x_kernel, "x", orders + [((512, 128), F32)], 5, 1 << 31)(
        pos, tokens, z1, z2, z3, got_a
    )
    a4, qfar_a, qfar_b, got_b, got_q, xa, xb, squares = lax.optimization_barrier(
        (a4, qfar_a, qfar_b, got_b, got_q, xa, xb, squares)
    )
    q_parts = (qst, qright, qleft, qfar_a, qfar_b)

    flops = 2 * 512 * 4096 * 1024
    kv_rows, r, part, give, xa, xb = kernel(
        kv_kernel,
        "kv",
        [
            ((2, 512, 512), BF),
            ((512, 128), F32),
            ((2, 128, 128), F32),
            ((2, 128, 128), BF),
        ]
        + orders,
        11,
        flops,
        aliases={1: 4, 2: 5},
    )(pos, xa, xb, squares, a4, st, right, left, far_a, far_b, got_a, got_b)
    q_other = (got_q, swap(cat([qfar_a, qfar_b])))
    (query,) = kernel(q_kernel, "q", [((512, 512), BF)], 10, flops // 2)(
        pos, xa, xb, *q_parts, *q_other, r
    )
    (raw,) = kernel(block_kernel, "block", [((512, 512), F32)], 3, flops // 2)(
        pos, query, kv_rows, carried
    )

    heads = (2, 128, 128)
    from_sib = swap(give)
    (sent,) = kernel(chip_kernel, "chip", [(heads, BF)], 2, 1 << 16)(
        pos, part, from_sib
    )
    near = [by_y(sent, k) for k in (1, -1, 2)]
    near[0] = after(near[0], query)
    before, row = kernel(row_kernel, "row", [(heads, F32), (heads, BF)], 4, 1 << 16)(
        pos, sent, *near
    )
    near = [by_x(row, k) for k in (1, -1, 2)]
    before = after(before, raw)
    both = (2,) + heads
    mine, give = kernel(plane_kernel, "plane", [(both, F32), (both, F32)], 7, 1 << 16)(
        pos, row, *near, before, part, from_sib
    )
    return kernel(out_kernel, "out", [((512, 512), BF), ((4, 128, 128), F32)], 6, 1 << 28)(
        pos, query, raw, mine, swap(give), carried, out_gain.reshape(1, 512)
    )


def solution(mesh):
    return jax.shard_map(
        shards,
        mesh=mesh,
        in_specs=(
            P("seq", "tensor"),
            P(),
            P("seq", "tensor"),
            P("seq", "tensor"),
            P("seq", "tensor"),
            P("tensor"),
            P("tensor", None, None),
        ),
        out_specs=(P("seq", "tensor"), P("tensor", None, None)),
        check_vma=False,
    )
```

```python
import jax
import jax.numpy as jnp
from jax import lax
from jax.experimental import pallas as pl
from jax.experimental.pallas import tpu as pltpu
from jax.sharding import PartitionSpec as P

NX, NY, NC, NZ = 4, 4, 2, 8
BOTH = ("seq", "tensor")
BF, F32 = jnp.bfloat16, jnp.float32


def place(x, y, c, z):
    return (((x % NX) * NY + y % NY) * NC + c % NC) * NZ + z % NZ


def move(a, f):
    pairs = [
        (place(x, y, c, z), place(*f(x, y, c, z)))
        for x in range(NX)
        for y in range(NY)
        for c in range(NC)
        for z in range(NZ)
    ]
    return lax.ppermute(a, BOTH, pairs)


def swap(a):
    return move(a, lambda x, y, c, z: (x, y, c + 1, z))


def along_z(a):
    return move(a, lambda x, y, c, z: (x, y, c, z + (1 if c == 0 else -1)))


def first(a, k):
    return move(a, lambda x, y, c, z: (x + k, y, c, z) if c == 0 else (x, y + k, c, z))


def second(a, k):
    return move(a, lambda x, y, c, z: (x, y + k, c, z) if c == 0 else (x + k, y, c, z))


def by_x(a, k):
    return move(a, lambda x, y, c, z: (x + k, y, c, z))


def by_y(a, k):
    return move(a, lambda x, y, c, z: (x, y + k, c, z))


def scalars(pos):
    return pos[0], pos[1], pos[2], pos[3]


def slot_of(step):
    step = lax.rem(step + 4, 4)
    return jnp.where(step >= 2, 5 - step, step)


def column(c, x, y, q):
    dx, dy = slot_of(x - q // NY), slot_of(y - lax.rem(q, NY))
    return jnp.where(c == 0, dy * 4 + dx, dx * 4 + dy)


def weights_dot(x_ref, parts, lanes):
    acc = None
    at = 0
    for part, n in parts:
        d = jnp.dot(x_ref[:, at : at + n], part[:n, lanes], preferred_element_type=F32)
        acc = d if acc is None else acc + d
        at += n
    return acc


def x_pass(pos, pieces, xa_ref, xb_ref, total):
    x, y, z, c = scalars(pos)
    for piece, lo, k in pieces:
        at = lax.rem(z + (1 - 2 * c) * k + 2 * NZ, NZ)
        for h in range(2):
            q = 2 * at + h
            block = piece[lo : lo + 512, h * 256 : (h + 1) * 256]
            xa_ref[:, pl.ds(pl.multiple_of(column(c, x, y, q) * 256, 256), 256)] = block
            xb_ref[:, pl.ds(pl.multiple_of(column(1 - c, x, y, q) * 256, 256), 256)] = block
            wide = block.astype(F32)
            wide = wide * wide
            total = total + wide[:, :128] + wide[:, 128:]
    return total


def x_kernel(pos, own, z1, z2, z3, got_a, xa_ref, xb_ref, squares_ref):
    pieces = ((own, 0, 0), (z1, 0, -1), (z2, 0, -2), (z3, 0, -3), (got_a, 1024, 1))
    squares_ref[...] = x_pass(pos, pieces, xa_ref, xb_ref, jnp.zeros((512, 128), F32))


def kv_kernel(pos, xa_in, xb_in, squares, a4, st, right, left, far_a, far_b, got_a, got_b, *outs):
    kv_ref, r_ref, part_ref, give_ref, xa_ref, xb_ref = outs
    c = pos[3]
    mine = ((st, 1024), (right, 1024), (left, 1024), (far_a, 512), (far_b, 512))
    other = ((got_a, 1024), (got_b, 3072))
    pieces = ((a4, 0, -4), (got_b, 3072, 2), (got_b, 3584, 3))
    total = x_pass(pos, pieces, xa_ref, xb_ref, squares[...])
    r = lax.rsqrt(jnp.sum(total, axis=1, keepdims=True) * (1.0 / 4096) + 1e-05)
    r_ref[...] = jnp.broadcast_to(r, (512, 128))

    @pl.loop(0, 2)
    def _(i):
        lanes = pl.ds(pl.multiple_of(i * 256, 256), 256)
        kv_ref[c, :, lanes] = (weights_dot(xa_ref, mine, lanes) * r_ref[:, :1]).astype(BF)
        kv_ref[1 - c, :, lanes] = (weights_dot(xb_ref, other, lanes) * r_ref[:, :1]).astype(BF)

    @pl.loop(0, 4)
    def _(h):
        head = lax.rem(h + 2 * c, 4)
        lanes = pl.ds(pl.multiple_of(head * 128, 128), 128)
        state = lax.dot_general(
            kv_ref[0, :, lanes],
            kv_ref[1, :, lanes],
            (((0,), (0,)), ((), ())),
            preferred_element_type=F32,
        )

        @pl.when(h < 2)
        def _():
            part_ref[h] = state

        @pl.when(h >= 2)
        def _():
            give_ref[h - 2] = state.astype(BF)


def chip_kernel(pos, part_ref, sib_ref, sent_ref):
    sent_ref[...] = (part_ref[...] + sib_ref[...].astype(F32)).astype(BF)


def along(at, sent, behind, ahead, opposite):
    b, f, o = behind[...].astype(F32), ahead[...].astype(F32), opposite[...].astype(F32)
    total = (sent[...].astype(F32) + o) + (b + f)
    before = jnp.where(at >= 1, b, 0.0) + jnp.where(at >= 2, o, 0.0) + jnp.where(at == 3, f, 0.0)
    return before, total


def row_kernel(pos, sent, behind, ahead, opposite, before_ref, next_ref):
    before, total = along(pos[1], sent, behind, ahead, opposite)
    before_ref[...] = before
    next_ref[...] = total.astype(BF)


def plane_kernel(pos, sent, behind, ahead, opposite, row_ref, part_ref, sib_ref, mine_ref, both_ref):
    before, total = along(pos[0], sent, behind, ahead, opposite)
    before = before + row_ref[...]
    c = pos[3]
    mine_ref[0] = before + jnp.where(c == 1, sib_ref[...].astype(F32), 0.0)
    mine_ref[1] = total
    both_ref[0] = before + jnp.where(c == 0, part_ref[...], 0.0)
    both_ref[1] = total


def split_dot(q, m):
    hi = m.astype(BF)
    lo = (m - hi.astype(F32)).astype(BF)
    return jnp.dot(q, hi, preferred_element_type=F32) + jnp.dot(q, lo, preferred_element_type=F32)


def q_kernel(pos, xa_ref, xb_ref, *refs):
    sizes = (1024, 1024, 1024, 512, 512, 3072, 1024)
    parts = tuple(zip(refs[:7], sizes))
    mine, other = parts[:5], parts[5:]
    r_ref, q_ref = refs[7:]
    c = pos[3]
    for x_ref, parts, to in ((xa_ref, mine, c), (xb_ref, other, 1 - c)):
        got = weights_dot(x_ref, parts, slice(0, 256)) * r_ref[:, :1]
        q_ref[:, pl.ds(pl.multiple_of(to * 256, 256), 256)] = got.astype(BF)


def block_kernel(pos, q_ref, kv_ref, carried_ref, raw_ref):
    row = lax.broadcasted_iota(jnp.int32, (512, 512), 0)
    col = lax.broadcasted_iota(jnp.int32, (512, 512), 1)

    @pl.loop(0, 4)
    def _(h):
        lanes = pl.ds(pl.multiple_of(h * 128, 128), 128)
        q = q_ref[:, lanes]
        scores = lax.dot_general(
            q, kv_ref[0, :, lanes], (((1,), (1,)), ((), ())), preferred_element_type=F32
        )
        weights = jnp.where(col <= row, scores, 0.0).astype(BF)
        intra = jnp.dot(weights, kv_ref[1, :, lanes], preferred_element_type=F32)
        raw_ref[:, lanes] = intra + split_dot(q, carried_ref[h])


def out_kernel(pos, q_ref, raw_ref, mine_ref, both_ref, carried_ref, gain_ref, out_ref, final_ref):
    c = pos[3]
    for own in range(2):
        for n in range(2):
            h = 2 * (c if own else 1 - c) + n
            lanes = pl.ds(pl.multiple_of(h * 128, 128), 128)
            before = mine_ref[0, n] if own else both_ref[0, n]
            total = mine_ref[1, n] if own else both_ref[1, n]
            raw = raw_ref[:, lanes] + split_dot(q_ref[:, lanes], before)
            scale = lax.rsqrt(jnp.mean(raw * raw, axis=1, keepdims=True) + 1e-06)
            out_ref[:, lanes] = (raw * scale * gain_ref[:, lanes]).astype(BF)
            final_ref[h] = carried_ref[h] + total


SMEM = pl.BlockSpec(memory_space=pltpu.SMEM)
VMEM = pl.BlockSpec(memory_space=pltpu.VMEM)


def kernel(body, name, outs, n_in, flops, space=VMEM, scratch=(), aliases=None, size=8):
    return pl.pallas_call(
        body,
        name=name,
        out_shape=tuple(jax.ShapeDtypeStruct(*o) for o in outs),
        in_specs=[SMEM] + (space if isinstance(space, list) else [space] * n_in),
        out_specs=(VMEM,) * len(outs),
        input_output_aliases=aliases or {},
        scratch_shapes=scratch,
        compiler_params=pltpu.CompilerParams(vmem_limit_bytes=size << 20),
        cost_estimate=pl.CostEstimate(flops=flops, bytes_accessed=1 << 20, transcendentals=0),
    )


def after(a, *deps):
    return lax.optimization_barrier((a,) + deps)[0]


def shards(tokens, norm_gain, w_query, w_key, w_value, out_gain, carried):
    s = lax.axis_index("seq").astype(jnp.int32)
    z = lax.axis_index("tensor").astype(jnp.int32)
    c = lax.rem(s, 2)
    y = lax.rem(s // 2, NY)
    x = s // (2 * NY)
    pos = jnp.stack([x, y, z, c])
    tokens, pos = lax.optimization_barrier((tokens, pos))
    even = c == 0
    pick = lambda a, b: jnp.where(even, a, b)

    sib = swap(tokens)
    mine = jnp.concatenate([pick(w_key, w_value), pick(w_query[:, :256], w_query[:, 256:])], 1)
    give = jnp.concatenate([pick(w_value, w_key), pick(w_query[:, 256:], w_query[:, :256])], 1)
    got = swap(after(give, sib))
    g = lax.dynamic_slice(norm_gain, ((s // 2) * 256,), (256,))[:, None]
    chip = jnp.concatenate([pick(mine, got), pick(got, mine)], 0)
    chip = (chip.astype(F32) * g).astype(BF)
    cat = jnp.concatenate
    z1 = along_z(after(cat([tokens, sib]), got))
    near = [first(chip, k) for k in (1, -1, 2)]
    z1, *near = lax.optimization_barrier((z1, *near))
    near = [chip] + near
    st = cat([w[:, :512] for w in near])
    qst = cat([w[:, 512:] for w in near])
    z2 = along_z(z1)
    right, left = second(st, 1), second(st, -1)
    got_a = swap(cat([st, z1[512:]]))
    z2, right, left, got_a = lax.optimization_barrier((z2, right, left, got_a))
    z3 = along_z(z2)
    far_a, far_b = second(right[:512], 1), second(left[512:], -1)
    qright, qleft = second(qst, 1), second(qst, -1)
    z3, far_a, far_b, qright, qleft = lax.optimization_barrier((z3, far_a, far_b, qright, qleft))
    a4 = along_z(z3[:512])
    qfar_a, qfar_b = second(qright[:512], 1), second(qleft[512:], -1)
    got_b = swap(cat([right, left, far_a, far_b, z2[512:], z3[512:]]))
    got_q = swap(cat([qst, qright, qleft]))
    orders = [((512, 4096), BF), ((512, 4096), BF)]
    xa, xb, squares = kernel(x_kernel, "x", orders + [((512, 128), F32)], 5, 1 << 31)(
        pos, tokens, z1, z2, z3, got_a
    )
    a4, got_b, xa, xb, squares = lax.optimization_barrier((a4, got_b, xa, xb, squares))
    q_parts = (qst, qright, qleft, qfar_a, qfar_b)

    flops = 2 * 512 * 4096 * 1024
    kv_rows, r, part, give, xa, xb = kernel(
        kv_kernel,
        "kv",
        [
            ((2, 512, 512), BF),
            ((512, 128), F32),
            ((2, 128, 128), F32),
            ((2, 128, 128), BF),
        ]
        + orders,
        11,
        flops,
        aliases={1: 4, 2: 5},
    )(pos, xa, xb, squares, a4, st, right, left, far_a, far_b, got_a, got_b)
    q_other = (got_q, swap(cat([after(qfar_a, part), after(qfar_b, part)])))
    (query,) = kernel(q_kernel, "q", [((512, 512), BF)], 10, flops // 2)(
        pos, xa, xb, *q_parts, *q_other, r
    )
    (raw,) = kernel(block_kernel, "block", [((512, 512), F32)], 3, flops // 2)(
        pos, query, kv_rows, carried
    )

    heads = (2, 128, 128)
    from_sib = swap(give)
    (sent,) = kernel(chip_kernel, "chip", [(heads, BF)], 2, 1 << 16)(
        pos, part, from_sib
    )
    near = [by_y(sent, k) for k in (1, -1, 2)]
    near[0] = after(near[0], query)
    before, row = kernel(row_kernel, "row", [(heads, F32), (heads, BF)], 4, 1 << 16)(
        pos, sent, *near
    )
    near = [by_x(row, k) for k in (1, -1, 2)]
    before = after(before, raw)
    both = (2,) + heads
    mine, give = kernel(plane_kernel, "plane", [(both, F32), (both, F32)], 7, 1 << 16)(
        pos, row, *near, before, part, from_sib
    )
    return kernel(out_kernel, "out", [((512, 512), BF), ((4, 128, 128), F32)], 6, 1 << 28)(
        pos, query, raw, mine, swap(give), carried, out_gain.reshape(1, 512)
    )


def solution(mesh):
    return jax.shard_map(
        shards,
        mesh=mesh,
        in_specs=(
            P("seq", "tensor"),
            P(),
            P("seq", "tensor"),
            P("seq", "tensor"),
            P("seq", "tensor"),
            P("tensor"),
            P("tensor", None, None),
        ),
        out_specs=(P("seq", "tensor"), P("tensor", None, None)),
        check_vma=False,
    )
```
